32 devices in a mesh: ctx: 4 (over y, x), exp: 8 (over z, core).
Axes of the slice: x: 2, y: 2, z: 4, core: 2. Of those that a mesh axis runs over, the one named last changes fastest.
Arguments:
- residual_in: bfloat16 [1024, 4096], P(('ctx', 'exp')), may hold values from -6 to 6
- query_rows: bfloat16 [1024, 4096], P('ctx', 'exp'), may hold values from -6 to 6
- key_rows: bfloat16 [1024, 4096], P('ctx', 'exp'), may hold values from -6 to 6
- value_rows: bfloat16 [1024, 4096], P('ctx', 'exp'), may hold values from -6 to 6
- log_decay: float32 [1024, 32], P('ctx', 'exp'), may hold values from -3 to 0
- attn_gain: float32 [4096], P('exp'), may hold values from 0.5 to 1.5
- moe_gain: float32 [4096], replicated, may hold values from 0.5 to 1.5
- expert_ids: int32 [1024, 2], P(('ctx', 'exp')), may hold values from 0 to 7, all different within a row; in each aligned block of 32 rows (0 to 31, 32 to 63, ...) at most 12 rows name the same one
- route_weight: float32 [1024, 2], P(('ctx', 'exp')), may hold values from 0.1 to 1
- gate_weight: bfloat16 [8, 4096, 4608], P('exp', None, 'ctx'), may hold values from -0.09375 to 0.09375
- up_weight: bfloat16 [8, 4096, 4608], P('exp', None, 'ctx'), may hold values from -0.09375 to 0.09375
- down_weight: bfloat16 [8, 4608, 4096], P('exp', 'ctx'), may hold values from -0.09375 to 0.09375
Outputs:
- layer_out: bfloat16 [1024, 4096], P(('ctx', 'exp'))
The draws below stay inside these ranges and needn't reach their ends.
Inputs may be any that keep to these rules, and one draw needn't show every extreme that they name: `expert_ids`: each token names two different experts; in the rows of one device no expert is named by more than 12 tokens, a bound that some block reaches.
All inputs are finite; a program needn't handle non-finite values.
Results may differ from the reference program's by a relative error of at most 0.012.
Values may be sent and summed in bfloat16 or wider, within the bound.
No kernel may reach another device: no remote copies, remote signals or barrier semaphores. Data moves between devices by JAX's collectives and lax.ppermute only.
A program may use at most 128 MiB of HBM per device.

```python
import math
import jax
import jax.numpy as jnp
import numpy as np
from jax import lax

HEAD = 128
HEADS = 32
D = 4096
FF = 4608
TOPK = 2
SPAN = 256
SEQUENCE_TOKENS = 1024
TOK_DEV = 32
EXPERTS = 8
CAP = 12
N_CTX = 4


def draw_log_decay(key, part):
    random_subkeys = jax.random.split(jax.random.fold_in(key, 17), 6)
    fast_share = 0.5
    choose = jax.random.uniform(random_subkeys[0], (HEADS,), jnp.float32)
    fast_rate = jnp.exp(jax.random.uniform(random_subkeys[1], (HEADS,), jnp.float32, math.log(1.0 / 50.0), math.log(1.0 / 30.0)))
    slow_rate = jnp.exp(jax.random.uniform(random_subkeys[2], (HEADS,), jnp.float32, math.log(0.05 / SEQUENCE_TOKENS), math.log(0.5 / SEQUENCE_TOKENS)))
    baseline_rate = jnp.where(choose < fast_share, fast_rate, slow_rate)
    coarse_noise = jax.random.uniform(random_subkeys[3], (SEQUENCE_TOKENS, HEADS), jnp.float32, 0.5, 1.5)
    spike_positions = jax.random.randint(random_subkeys[4], (4,), 0, SEQUENCE_TOKENS)
    spike_drops = jnp.log(jax.random.uniform(random_subkeys[5], (4,), jnp.float32, 0.5, 0.8))
    spike_hits = (jnp.arange(SEQUENCE_TOKENS)[:, None] == spike_positions[None, :]).astype(jnp.float32)
    spike_sum = jnp.sum(spike_hits * spike_drops[None, :], axis=1)
    return (spike_sum[:, None] - baseline_rate[None, :] * coarse_noise).astype(jnp.float32)


def levels(rng, dims, shards, smallest, largest):
    def one(axis_at, blocks):
        heights = jax.random.uniform(jax.random.fold_in(jax.random.fold_in(rng, 6), axis_at), (blocks,), jnp.float32, smallest / len(shards), largest / len(shards))
        return jnp.repeat(jnp.exp(heights), dims[axis_at] // blocks).reshape((-1,) + (1,) * (len(dims) - axis_at - 1))

    level = one(*shards[0])
    for cut in shards[1:]:
        level = level * one(*cut)
    return level


def shared_out(stream_key, own, number, rows, amount, top, reach, skew):
    sequence = jax.random.permutation(stream_key, amount)
    packed, common = shares(amount, rows * top, reach, skew, True), shares(amount, rows * top, reach, skew, False)
    places = jnp.arange(amount)

    def named(lengths, turn):
        used = int((lengths > 0).sum())
        fixed = max(1, used // 4)
        moved = fixed + (places - fixed + turn * (used - fixed)) % max(1, amount - fixed)
        return jnp.zeros((amount,), jnp.int32).at[sequence[jnp.where(places < fixed, places, moved)]].set(jnp.asarray(lengths, jnp.int32))

    lengths = jnp.where(number % 4 == 0, named(packed, number // 4), named(common, number - number // 4 - 1))
    mixed = jax.random.permutation(jax.random.fold_in(own, 3), amount)
    source_of, sink = mixed[0:amount // 2 * 2:2], mixed[1:amount // 2 * 2:2]
    room = jnp.minimum(lengths[source_of] - 1, reach - lengths[sink]) // 2
    room = jnp.where((source_of == sequence[0]) | (sink == sequence[0]) | (lengths[sink] == 0), 0, jnp.maximum(room, 0))
    moved = jax.random.randint(jax.random.fold_in(own, 4), (amount // 2,), 0, 1 << 20) % (room + 1)
    lengths = lengths.at[source_of].add(-moved).at[sink].add(moved)
    items = jnp.searchsorted(jnp.cumsum(lengths), jnp.arange(rows * top), side="right").astype(jnp.int32)
    table = items.reshape(top, rows).T
    table = table[jax.random.permutation(jax.random.fold_in(own, 1), rows)]
    turn = jax.random.randint(jax.random.fold_in(own, 2), (rows, 1), 0, top)
    return jnp.take_along_axis(table, (jnp.arange(top)[None, :] + turn) % top, axis=1)


def shares(amount, total, reach, lean, full):
    loads = [(1 << 20) // math.isqrt(standing ** lean) + 1 for standing in range(1, amount + 1)]
    largest = reach if full else min(reach, max(-(-total // amount), total * loads[0] // sum(loads)))
    least = 1 if total - largest >= amount - 1 else 0
    counts, spare = [largest] + [least] * (amount - 1), total - largest - least * (amount - 1)
    while spare > 0:
        free = [i for i in range(1, amount) if counts[i] < largest] or [i for i in range(1, amount) if counts[i] < reach]
        pool, left = sum([loads[i] for i in free]), spare
        for i in free:
            extra = min(reach - counts[i], max(1, left * loads[i] // pool), spare)
            counts[i] = counts[i] + extra
            spare = spare - extra
    return np.array(counts)


def gaussian(own_key, dims, scale, limit, shards=(), kind=jnp.bfloat16):
    factor_of = levels(own_key, dims, shards, -0.22, 0.18) if shards else 1.0
    values = jax.random.normal(own_key, dims, jnp.float32) * scale * factor_of
    return jnp.minimum(jnp.maximum(values, -limit), limit).astype(kind)


def setup_inputs(seed: int = 0) -> dict:
    keys = jax.random.split(jax.random.key(seed), 13)
    residual_in = gaussian(keys[0], (SEQUENCE_TOKENS, D), 1.0, 6.0, ((0, 32),))
    query_rows = gaussian(keys[1], (SEQUENCE_TOKENS, D), 1.0, 6.0, ((0, 4), (1, 8)))
    key_rows = gaussian(keys[2], (SEQUENCE_TOKENS, D), 1.0, 6.0, ((0, 4), (1, 8)))
    value_rows = gaussian(keys[3], (SEQUENCE_TOKENS, D), 1.0, 6.0, ((0, 4), (1, 8)))
    log_decay = draw_log_decay(jax.random.fold_in(keys[12], 71), 0)
    attn_gain = jnp.clip(1.0 + 0.1 * jax.random.normal(keys[5], (D,), jnp.float32), 0.5, 1.5)
    moe_gain = jnp.clip(1.0 + 0.1 * jax.random.normal(keys[6], (D,), jnp.float32), 0.5, 1.5)
    expert_ids_keys = jax.random.split(jax.random.fold_in(keys[7], 1), SEQUENCE_TOKENS // TOK_DEV)
    expert_ids_turns = jax.random.permutation(jax.random.fold_in(keys[7], 3), SEQUENCE_TOKENS // TOK_DEV)
    expert_ids = jax.vmap(lambda own, number: shared_out(jax.random.fold_in(keys[7], 2), own, number, TOK_DEV, EXPERTS, TOPK, CAP, 2))(expert_ids_keys, expert_ids_turns).reshape((SEQUENCE_TOKENS, TOPK))
    route_weight = jnp.clip(0.1 + 0.9 * jax.random.uniform(keys[8], (SEQUENCE_TOKENS, TOPK), jnp.float32) ** levels(keys[8], (SEQUENCE_TOKENS, TOPK), ((0, 32),), -0.2, 0.2), 0.1, 1.0)
    gate_weight = gaussian(keys[9], (EXPERTS, D, FF), D ** -0.5, 0.09375, ((0, 8), (2, 4)))
    up_weight = gaussian(keys[10], (EXPERTS, D, FF), D ** -0.5, 0.09375, ((0, 8), (2, 4)))
    down_weight = gaussian(keys[11], (EXPERTS, FF, D), FF ** -0.5, 0.09375, ((0, 8), (1, 4)))
    return {"residual_in": residual_in, "query_rows": query_rows, "key_rows": key_rows, "value_rows": value_rows, "log_decay": log_decay, "attn_gain": attn_gain, "moe_gain": moe_gain, "expert_ids": expert_ids, "route_weight": route_weight, "gate_weight": gate_weight, "up_weight": up_weight, "down_weight": down_weight}


EPSILON = 1e-05

def round_bf16(tensor):
    return lax.optimization_barrier(tensor.astype(jnp.bfloat16)).astype(jnp.float32)

def attention_block(state, block):
    query_blk, key_blk, value_blk, decay_blk = block
    query_f = query_blk.astype(jnp.float32)
    key_f = key_blk.astype(jnp.float32)
    value_f = value_blk.astype(jnp.float32)
    cumulative = jnp.cumsum(decay_blk, axis=0)
    block_total = cumulative[-1]
    length = decay_blk.shape[0]
    causal = jnp.arange(length)[:, None] >= jnp.arange(length)[None, :]
    spread = cumulative.T[:, :, None] - cumulative.T[:, None, :]
    decay_mask = jnp.exp(jnp.where(causal[None], spread, -jnp.inf))
    scores = jnp.einsum('thd,shd->hts', query_f, key_f)
    attend_weight = round_bf16(scores * decay_mask)
    within = jnp.einsum('hts,shd->thd', attend_weight, value_f)
    carried = jnp.exp(cumulative)[:, :, None] * jnp.einsum('thd,hde->the', query_f, round_bf16(state))
    weighted = round_bf16(key_f * jnp.exp(block_total - cumulative)[:, :, None])
    update = jnp.einsum('thd,the->hde', weighted, value_f)
    new_state = jnp.exp(block_total)[:, None, None] * state + update
    return (new_state, carried + within)

def expert_apply(operands):
    rows_in, gate_mat, up_mat, down_mat = operands
    slice_width = FF // N_CTX
    gate_slices = gate_mat.reshape(D, N_CTX, slice_width).transpose(1, 0, 2)
    up_slices = up_mat.reshape(D, N_CTX, slice_width).transpose(1, 0, 2)
    down_slices = down_mat.reshape(N_CTX, slice_width, D)

    def add_slice(running, slices):
        gate_val = jnp.dot(rows_in, slices[0], preferred_element_type=jnp.float32)
        up_val = jnp.dot(rows_in, slices[1], preferred_element_type=jnp.float32)
        hidden_act = (jax.nn.silu(gate_val) * up_val).astype(jnp.bfloat16)
        slice_part = round_bf16(jnp.dot(hidden_act, slices[2], preferred_element_type=jnp.float32))
        return (running + slice_part, None)
    start_sum = jnp.zeros((rows_in.shape[0], D), jnp.float32)
    summed, _ = lax.scan(add_slice, start_sum, (gate_slices, up_slices, down_slices))
    return summed.astype(jnp.bfloat16)

def reference(residual_in, query_rows, key_rows, value_rows, log_decay, attn_gain, moe_gain, expert_ids, route_weight, gate_weight, up_weight, down_weight):
    blocks = SEQUENCE_TOKENS // SPAN
    block_shape = (blocks, SPAN, HEADS, HEAD)
    start_state = jnp.zeros((HEADS, HEAD, HEAD), jnp.float32)
    _, raw_out = lax.scan(attention_block, start_state, (query_rows.reshape(block_shape), key_rows.reshape(block_shape), value_rows.reshape(block_shape), log_decay.reshape(blocks, SPAN, HEADS)))
    raw_out = raw_out.reshape(SEQUENCE_TOKENS, HEADS, HEAD)
    scale_rms = lax.rsqrt(lax.optimization_barrier(jnp.mean(raw_out * raw_out, axis=-1, keepdims=True)) + EPSILON)
    head_out = (raw_out * scale_rms * attn_gain.reshape(HEADS, HEAD)).astype(jnp.bfloat16).reshape(SEQUENCE_TOKENS, D)
    hidden_state = residual_in.astype(jnp.float32) + head_out.astype(jnp.float32)
    normed = (hidden_state * lax.rsqrt(lax.optimization_barrier(jnp.mean(hidden_state * hidden_state, axis=-1, keepdims=True)) + EPSILON) * moe_gain).astype(jnp.bfloat16)
    groups = SEQUENCE_TOKENS // TOK_DEV
    pair_count = TOK_DEV * TOPK
    flat_ids = expert_ids.reshape(groups, pair_count).astype(jnp.int32)
    one_hot = (flat_ids[:, :, None] == jnp.arange(EXPERTS, dtype=jnp.int32)[None, None, :]).astype(jnp.int32)
    before = jnp.cumsum(one_hot, axis=1) - one_hot
    slot_index = lax.optimization_barrier(jnp.sum(before * one_hot, axis=2))
    target = (flat_ids * CAP + slot_index).astype(jnp.int32)
    pair_rows = jnp.broadcast_to(normed.reshape(groups, TOK_DEV, 1, D), (groups, TOK_DEV, TOPK, D)).reshape(groups, pair_count, D)
    owner = jnp.broadcast_to(jnp.arange(groups, dtype=jnp.int32)[:, None], (groups, pair_count))
    buffer = jnp.zeros((groups, EXPERTS * CAP, D), normed.dtype).at[owner, target].set(pair_rows)
    per_expert = buffer.reshape(groups, EXPERTS, CAP, D).transpose(1, 0, 2, 3).reshape(EXPERTS, groups * CAP, D)
    expert_out = lax.map(expert_apply, (per_expert, gate_weight, up_weight, down_weight))
    returned_rows = expert_out.reshape(EXPERTS, groups, CAP, D).transpose(1, 0, 2, 3).reshape(groups, EXPERTS * CAP, D)
    picked = jnp.take_along_axis(returned_rows, target[:, :, None], axis=1).astype(jnp.float32)
    picked = picked.reshape(SEQUENCE_TOKENS, TOPK, D)
    contrib = lax.optimization_barrier(jnp.sum(picked * route_weight[:, :, None], axis=1))
    return (hidden_state + contrib).astype(jnp.bfloat16)
```

```python
import functools

import jax
import jax.numpy as jnp
from jax import lax
from jax.experimental import pallas as pl
from jax.experimental.pallas import tpu as pltpu
from jax.sharding import PartitionSpec as P

HEAD = 128
EPSILON = 1e-05
F32 = jnp.float32
BF16 = jnp.bfloat16
LANES = 128
MIB = 2**20


def swap(x, axis, bits):
    n = lax.axis_size(axis)
    return lax.ppermute(x, axis, [(i, i ^ bits) for i in range(n)])


def call(kernel, outs, *args, scratch=(), any_args=(), vmem=24, flops=0, nbytes=0):
    specs = [
        pl.BlockSpec(memory_space=pl.ANY if i in any_args else pltpu.VMEM)
        for i in range(len(args))
    ]
    return pl.pallas_call(
        kernel,
        out_shape=tuple(jax.ShapeDtypeStruct(s, d) for s, d in outs),
        in_specs=specs,
        out_specs=tuple(pl.BlockSpec(memory_space=pltpu.VMEM) for _ in outs),
        scratch_shapes=list(scratch),
        compiler_params=pltpu.CompilerParams(vmem_limit_bytes=vmem * MIB),
        cost_estimate=pl.CostEstimate(flops=flops, bytes_accessed=nbytes, transcendentals=0),
    )(*args)


def bit_order(n, turn):
    count = n.bit_length() - 1
    return [(i + turn) % count for i in range(count)] if count else []


def cum_column(decay_ref):
    length = decay_ref.shape[1]
    row = lax.broadcasted_iota(jnp.int32, (length, length), 0)
    col = lax.broadcasted_iota(jnp.int32, (length, length), 1)
    lower = (row >= col).astype(F32)
    return lax.dot_general(
        lower,
        decay_ref[...],
        (((1,), (1,)), ((), ())),
        precision=lax.Precision.HIGHEST,
        preferred_element_type=F32,
    )


def cum_row(decay_ref):
    length = decay_ref.shape[1]
    row = lax.broadcasted_iota(jnp.int32, (length, length), 0)
    col = lax.broadcasted_iota(jnp.int32, (length, length), 1)
    upper = (row <= col).astype(F32)
    return jnp.dot(
        decay_ref[...], upper, precision=lax.Precision.HIGHEST, preferred_element_type=F32
    )


def state_kernel(decay_ref, key_ref, value_ref, out_ref):
    heads = decay_ref.shape[0]
    cum = cum_column(decay_ref)
    length = cum.shape[0]
    line = lax.broadcasted_iota(jnp.int32, (out_ref.shape[0] - heads * HEAD, HEAD), 0)
    tail = jnp.zeros(line.shape, F32)
    for h in range(heads):
        part = slice(h * HEAD, (h + 1) * HEAD)
        here = cum[:, h : h + 1]
        total = here[length - 1 : length, :]
        weighted = (key_ref[:, part].astype(F32) * jnp.exp(total - here)).astype(BF16)
        out_ref[part, :] = lax.dot_general(
            weighted, value_ref[:, part], (((0,), (0,)), ((), ())), preferred_element_type=F32
        ).astype(BF16)
        wide = jnp.broadcast_to(total, line.shape)
        high = wide.astype(BF16).astype(F32)
        tail = jnp.where(line == 2 * h, high, jnp.where(line == 2 * h + 1, wide - high, tail))
    out_ref[heads * HEAD :, :] = tail.astype(BF16)


def within_kernel(decay_ref, query_ref, key_ref, value_ref, out_ref):
    heads, length = decay_ref.shape
    down = cum_column(decay_ref)
    along = cum_row(decay_ref)
    row = lax.broadcasted_iota(jnp.int32, (length, length), 0)
    col = lax.broadcasted_iota(jnp.int32, (length, length), 1)
    causal = row >= col
    for h in range(heads):
        part = slice(h * HEAD, (h + 1) * HEAD)
        scores = lax.dot_general(
            query_ref[:, part],
            key_ref[:, part],
            (((1,), (1,)), ((), ())),
            preferred_element_type=F32,
        )
        spread = down[:, h : h + 1] - along[h : h + 1, :]
        decay = jnp.exp(jnp.where(causal, spread, -1e30))
        out_ref[:, part] = jnp.dot(
            (scores * decay).astype(BF16), value_ref[:, part], preferred_element_type=F32
        )


def share_kernel(n_exp, ids_ref, ids_row_ref, route_ref, res_ref, *out_refs):
    rows = res_ref.shape[0]
    width = res_ref.shape[1] // n_exp
    me = lax.axis_index("exp")
    before = lax.broadcasted_iota(jnp.int32, (rows, rows), 0) > lax.broadcasted_iota(
        jnp.int32, (rows, rows), 1
    )
    lane = lax.broadcasted_iota(jnp.int32, (rows, LANES), 1)
    info = jnp.zeros((rows, LANES), F32)
    for k in range(2):
        mine = ids_ref[:, k : k + 1]
        count = jnp.zeros((rows, rows), F32)
        for other in range(2):
            same = (mine == ids_row_ref[other : other + 1, :]) & before
            count = count + same.astype(F32)
        slot = jnp.sum(count, axis=1, keepdims=True)
        weight = route_ref[:, k : k + 1]
        high = weight.astype(BF16).astype(F32)
        info = jnp.where(lane == k, mine.astype(F32), info)
        info = jnp.where(lane == 2 + k, slot, info)
        info = jnp.where(lane == 4 + k, high, info)
        info = jnp.where(lane == 6 + k, weight - high, info)
    info = info.astype(BF16)
    for rel in range(n_exp):
        start = pl.multiple_of((me ^ rel) * width, LANES)
        out_refs[rel][:, :width] = res_ref[:, pl.ds(start, width)]
        out_refs[rel][:, width:] = info


def hidden_kernel(n_ctx, n_exp, decay_ref, query_ref, within_ref, gain_ref, *refs):
    states = refs[: n_ctx - 1]
    shares = refs[n_ctx - 1 : n_ctx - 1 + n_exp]
    hid_ref, info_ref, res_ref = refs[n_ctx - 1 + n_exp :]
    heads = decay_ref.shape[0]
    width = heads * HEAD
    me = lax.axis_index("exp")
    block = lax.axis_index("ctx")
    rows = shares[0].shape[0]
    for rel in range(n_exp):
        start = pl.multiple_of((me ^ rel) * rows, 16)
        res_ref[pl.ds(start, rows), :] = shares[rel][:, :width]
        info_ref[pl.ds(start, rows), :] = shares[rel][:, width:]
    grow = jnp.exp(cum_column(decay_ref))
    tails = [s[heads * HEAD :, :].astype(F32) for s in states]
    for h in range(heads):
        part = slice(h * HEAD, (h + 1) * HEAD)
        totals = [t[2 * h : 2 * h + 1, :] + t[2 * h + 1 : 2 * h + 2, :] for t in tails]
        incoming = jnp.zeros((HEAD, HEAD), F32)
        for a in range(1, n_ctx):
            log_weight = jnp.zeros((1, HEAD), F32)
            for b in range(1, n_ctx):
                if b != a:
                    between = ((block ^ b) > (block ^ a)) & ((block ^ b) < block)
                    log_weight = log_weight + totals[b - 1] * jnp.where(between, 1.0, 0.0)
            weight = jnp.exp(log_weight) * jnp.where((block ^ a) < block, 1.0, 0.0)
            incoming = incoming + weight * states[a - 1][part, :].astype(F32)
        carried = grow[:, h : h + 1] * jnp.dot(
            query_ref[:, part], incoming.astype(BF16), preferred_element_type=F32
        )
        raw = carried + within_ref[:, part]
        scale = lax.rsqrt(jnp.mean(raw * raw, axis=-1, keepdims=True) + EPSILON)
        head_out = (raw * scale * gain_ref[:, part]).astype(BF16)
        hid_ref[:, part] = (res_ref[:, part].astype(F32) + head_out.astype(F32)).astype(BF16)


def pack_kernel(n_exp, capacity, tok_rows, hid_ref, other_ref, info_ref, *out_refs):
    nz = n_exp // 2
    *packs, weight_ref = out_refs
    length, width = hid_ref.shape
    slots = packs[0].shape[0]
    me = lax.axis_index("exp")
    info = info_ref[...].astype(F32)
    whole = info.astype(jnp.int32)
    home = lax.broadcasted_iota(jnp.int32, (length, 1), 0) // tok_rows
    lane = lax.broadcasted_iota(jnp.int32, (length, slots), 1)
    for z in range(nz):
        expert = me ^ (2 * z)
        rel = home ^ expert
        base = (rel & 1) * (nz * capacity) + (rel >> 1) * capacity
        chosen = []
        for k in range(2):
            place = jnp.where(whole[:, k : k + 1] == expert, base + whole[:, 2 + k : 3 + k], -1)
            chosen.append((lane == place).astype(F32))
        pick = (chosen[0] + chosen[1]).astype(BF16)
        dims = (((0,), (0,)), ((), ()))
        packs[z][:, :width] = lax.dot_general(
            pick, hid_ref[...], dims, preferred_element_type=F32
        ).astype(BF16)
        packs[z][:, width:] = lax.dot_general(
            pick, other_ref[...], dims, preferred_element_type=F32
        ).astype(BF16)
        if z == 0:
            weights = chosen[0] * (info[:, 4:5] + info[:, 6:7])
            weights = weights + chosen[1] * (info[:, 5:6] + info[:, 7:8])
            weight_ref[...] = lax.dot_general(
                weights,
                jnp.ones((length, LANES), F32),
                dims,
                precision=lax.Precision.HIGHEST,
                preferred_element_type=F32,
            )


def gate_kernel(n_ctx, piece, first, last, gain_ref, gate_ref, up_ref, *refs):
    rows_in = refs[:n_ctx]
    rest = refs[n_ctx:]
    if first:
        prev = None
    else:
        prev, rest = rest[:3], rest[3:]
    if last:
        act_ref, x_ref, gate_buf, up_buf, sem = rest
        outs = None
    else:
        outs = rest[:3]
        x_ref, gate_buf, up_buf, sem = rest[3:]
    me = lax.axis_index("exp")
    slots = rows_in[0].shape[0]
    width = rows_in[0].shape[1] // 2
    copies = []
    for c in range(2):
        start = pl.multiple_of((me ^ (2 * piece + c)) * width, LANES)
        for w_ref, buf, which in ((gate_ref, gate_buf, 0), (up_ref, up_buf, 1)):
            copy = pltpu.make_async_copy(
                w_ref.at[0, pl.ds(start, width), :], buf.at[c], sem.at[2 * c + which]
            )
            copy.start()
            copies.append(copy)
    squares = []
    for r in range(n_ctx):
        total = None
        for c in range(2):
            start = pl.multiple_of((me ^ (2 * piece + c)) * width, LANES)
            gain = gain_ref[:, pl.ds(start, width)]
            x = rows_in[r][:, c * width : (c + 1) * width].astype(F32)
            x_ref[c, r * slots : (r + 1) * slots, :] = (x * gain).astype(BF16)
            square = jnp.sum(x * x, axis=1, keepdims=True)
            total = square if total is None else total + square
        squares.append(jnp.broadcast_to(total, (slots, LANES)))
    for c in range(2):
        x = x_ref[c]
        copies[2 * c].wait()
        gate = jnp.dot(x, gate_buf[c], preferred_element_type=F32)
        gate_sum = gate if c == 0 else gate_sum + gate
        copies[2 * c + 1].wait()
        up = jnp.dot(x, up_buf[c], preferred_element_type=F32)
        up_sum = up if c == 0 else up_sum + up
    square_sum = jnp.concatenate(squares, axis=0)
    if prev is not None:
        gate_sum = gate_sum + prev[0][...]
        up_sum = up_sum + prev[1][...]
        square_sum = square_sum + prev[2][...]
    if last:
        model_width = gain_ref.shape[1]
        scale = lax.rsqrt(square_sum[:, :1] / model_width + EPSILON)
        gate_val = gate_sum * scale
        up_val = up_sum * scale
        act_ref[...] = (gate_val * jax.nn.sigmoid(gate_val) * up_val).astype(BF16)
    else:
        outs[0][...] = gate_sum
        outs[1][...] = up_sum
        outs[2][...] = square_sum


def down_kernel(piece, first_bit, n_ctx, chunks, act_ref, down_ref, send_ref, *refs):
    *keeps, buf, sem = refs
    slots = keeps[0].shape[0]
    width = buf.shape[-1]
    copies = []
    for j in range(chunks):
        start = (piece * chunks + j) * width
        copy = pltpu.make_async_copy(
            down_ref.at[0, :, pl.ds(start, width)], buf.at[j], sem.at[j]
        )
        copy.start()
        copies.append(copy)
    sends = [r for r in range(n_ctx) if r >> first_bit & 1]
    stays = [r for r in range(n_ctx) if not r >> first_bit & 1]
    for j in range(chunks):
        copies[j].wait()
        out = jnp.dot(act_ref[...], buf[j], preferred_element_type=F32).astype(BF16)
        cols = slice(j * width, (j + 1) * width)
        for i, r in enumerate(sends):
            send_ref[i * slots : (i + 1) * slots, cols] = out[r * slots : (r + 1) * slots, :]
        for i, r in enumerate(stays):
            keeps[i][:, cols] = out[r * slots : (r + 1) * slots, :]


def finish_kernel(n_exp, n_parts, terms, first_piece, weight_ref, *refs):
    nz = n_exp // 2
    rows_in = refs[:nz]
    parts = refs[nz : nz + terms * n_parts]
    own_ref, other_ref, rows_ref = refs[nz + terms * n_parts :]
    slots, cols = rows_in[0].shape
    width = cols // 2
    half = slots // 2
    me = lax.axis_index("exp")
    for z in range(nz):
        for c in range(2):
            rows_ref[2 * z + c] = rows_in[z][:, c * width : (c + 1) * width]
    weight = weight_ref[:, :1]
    for i in range(n_parts):
        for c in range(2):
            inner = slice(c * width, (c + 1) * width)
            total = parts[terms * i][:slots, inner].astype(F32)
            for j in range(1, terms):
                total = total + parts[terms * i + j][:slots, inner].astype(F32)
            block = 2 * (first_piece + i) + c
            hid = rows_ref[me ^ block].astype(F32)
            out = (total * weight + 0.5 * hid).astype(BF16)
            outer = slice(i * cols + c * width, i * cols + (c + 1) * width)
            own_ref[:, outer] = out[:half, :]
            other_ref[:, outer] = out[half:, :]


def turn_kernel(nz, capacity, own_ref, other_ref, *refs):
    *outs, both_ref = refs
    half = own_ref.shape[0]
    both_ref[:half, :] = own_ref[...]
    both_ref[half:, :] = other_ref[...]
    line = lax.broadcasted_iota(jnp.int32, (2 * half, 2 * half), 0)
    lane = lax.broadcasted_iota(jnp.int32, (2 * half, 2 * half), 1)
    core = lane // half
    z = (lane % half) // capacity
    s = (lane % half) % capacity
    pick = (line == z * (2 * capacity) + core * capacity + s).astype(BF16)
    moved = jnp.dot(pick, both_ref[...], preferred_element_type=F32).astype(BF16)
    for i in range(nz):
        outs[i][...] = moved[i * 2 * capacity : (i + 1) * 2 * capacity, :]


def home_kernel(nz, groups, capacity, ids_ref, share_ref, *refs):
    *pieces, out_ref = refs
    me = lax.axis_index("exp")
    tok_rows = out_ref.shape[0]
    cols = pieces[0].shape[1]
    width = share_ref.shape[1] - LANES
    info = share_ref[:, width:].astype(F32).astype(jnp.int32)
    lane = lax.broadcasted_iota(jnp.int32, (tok_rows, 2 * capacity), 1)
    picks = []
    for z in range(nz):
        pick = jnp.zeros(lane.shape, F32)
        for k in range(2):
            rel = info[:, k : k + 1] ^ me
            place = jnp.where((rel >> 1) == z, (rel & 1) * capacity + info[:, 2 + k : 3 + k], -1)
            pick = pick + (lane == place).astype(F32)
        picks.append(pick.astype(BF16))
    for g in range(groups):
        total = None
        for z in range(nz):
            term = jnp.dot(picks[z], pieces[g * nz + z][...], preferred_element_type=F32)
            total = term if total is None else total + term
        out_ref[:, g * cols : (g + 1) * cols] = total.astype(BF16)


def gather_ctx(piece, n_ctx, turn):
    held = {0: piece}
    for bit in bit_order(n_ctx, turn):
        for rel in sorted(held):
            held[rel ^ (1 << bit)] = swap(held[rel], "ctx", 1 << bit)
    return [held[r] for r in range(n_ctx)]


def body(
    residual_in,
    query_rows,
    key_rows,
    value_rows,
    log_decay,
    attn_gain,
    moe_gain,
    expert_ids,
    route_weight,
    gate_weight,
    up_weight,
    down_weight,
):
    n_ctx = lax.axis_size("ctx")
    n_exp = lax.axis_size("exp")
    nz = n_exp // 2
    length, width = query_rows.shape
    heads = width // HEAD
    tok_rows, model_width = residual_in.shape
    capacity = 3 * tok_rows // n_exp
    slots = n_exp * capacity
    hidden = gate_weight.shape[2]
    rows = n_ctx * slots
    decay = log_decay.T

    tail = -(-2 * heads // 16) * 16
    (state,) = call(
        state_kernel, [((heads * HEAD + tail, HEAD), BF16)], decay, key_rows, value_rows
    )
    states = [swap(state, "ctx", r) for r in range(1, n_ctx)]
    shares = call(
        functools.partial(share_kernel, n_exp),
        [((tok_rows, width + LANES), BF16)] * n_exp,
        expert_ids,
        expert_ids.T,
        route_weight,
        residual_in,
    )
    moved = [shares[0]] + [swap(shares[r], "exp", r) for r in range(1, n_exp)]
    (within,) = call(
        within_kernel, [((length, width), F32)], decay, query_rows, key_rows, value_rows
    )
    hid, info = call(
        functools.partial(hidden_kernel, n_ctx, n_exp),
        [((length, width), BF16), ((length, LANES), BF16)],
        decay,
        query_rows,
        within,
        attn_gain.reshape(1, width),
        *states,
        *moved,
        scratch=[pltpu.VMEM((length, width), BF16)],
    )
    hid_other = swap(hid, "exp", 1)
    *packs, row_weight = call(
        functools.partial(pack_kernel, n_exp, capacity, tok_rows),
        [((slots, 2 * width), BF16)] * nz + [((slots, LANES), F32)],
        hid,
        hid_other,
        info,
    )
    arrived = [packs[0]] + [swap(packs[z], "exp", 2 * z) for z in range(1, nz)]
    gathered = [gather_ctx(arrived[z], n_ctx, z) for z in range(nz)]

    gain = moe_gain.reshape(1, model_width)
    sums = ()
    for z in range(nz):
        last = z == nz - 1
        outs = (
            [((rows, hidden), BF16)]
            if last
            else [((rows, hidden), F32), ((rows, hidden), F32), ((rows, LANES), F32)]
        )
        sums = call(
            functools.partial(gate_kernel, n_ctx, z, z == 0, last),
            outs,
            gain,
            gate_weight,
            up_weight,
            *gathered[z],
            *sums,
            any_args=(1, 2),
            scratch=[
                pltpu.VMEM((2, rows, width), BF16),
                pltpu.VMEM((2, width, hidden), BF16),
                pltpu.VMEM((2, width, hidden), BF16),
                pltpu.SemaphoreType.DMA((4,)),
            ],
            vmem=36,
            flops=8 * rows * width * hidden,
            nbytes=8 * width * hidden,
        )
    (act,) = sums

    chunks = 2
    finished = []
    for p in range(nz):
        order = bit_order(n_ctx, p)
        stays = [r for r in range(n_ctx) if not r >> order[0] & 1]
        send, *keeps = call(
            functools.partial(down_kernel, p, order[0], n_ctx, chunks),
            [((rows // 2, 2 * width), BF16)] + [((slots, 2 * width), BF16)] * (n_ctx // 2),
            act,
            down_weight,
            any_args=(1,),
            scratch=[
                pltpu.VMEM((chunks, hidden, 2 * width // chunks), BF16),
                pltpu.SemaphoreType.DMA((chunks,)),
            ],
            flops=4 * rows * width * hidden,
            nbytes=4 * width * hidden,
        )
        got = swap(send, "ctx", 1 << order[0])
        held = {r: [keeps[i], got[i * slots : (i + 1) * slots]] for i, r in enumerate(stays)}
        held[0][1] = got
        for bit in order[1:]:
            moving = [r for r in sorted(held) if r >> bit & 1]
            outgoing = [
                functools.reduce(jnp.add, [t.astype(F32) for t in held.pop(r)]).astype(BF16)
                for r in moving
            ]
            packed = outgoing[0] if len(outgoing) == 1 else jnp.concatenate(outgoing, axis=0)
            got = swap(packed, "ctx", 1 << bit)
            for i, r in enumerate(moving):
                kept = r ^ (1 << bit)
                held[kept].append(got if kept == 0 else got[i * slots : (i + 1) * slots])
        finished.append(held[0])

    groups = 2
    per = nz // groups
    pieces = []
    for g in range(groups):
        parts = [t for p in range(g * per, (g + 1) * per) for t in finished[p]]
        terms = len(finished[0])
        own, other = call(
            functools.partial(finish_kernel, n_exp, per, terms, g * per),
            [((slots // 2, per * 2 * width), BF16)] * 2,
            row_weight,
            *arrived,
            *parts,
            scratch=[pltpu.VMEM((n_exp, slots, width), BF16)],
        )
        other = swap(other, "exp", 1)
        turned = call(
            functools.partial(turn_kernel, nz, capacity),
            [((2 * capacity, per * 2 * width), BF16)] * nz,
            own,
            other,
            scratch=[pltpu.VMEM((slots, per * 2 * width), BF16)],
        )
        pieces += [turned[0]] + [swap(turned[z], "exp", 2 * z) for z in range(1, nz)]
    (out,) = call(
        functools.partial(home_kernel, nz, groups, capacity),
        [((tok_rows, model_width), BF16)],
        expert_ids,
        shares[0],
        *pieces,
    )
    return out


def solution(mesh):
    in_specs = (
        P(("ctx", "exp"), None),
        P("ctx", "exp"),
        P("ctx", "exp"),
        P("ctx", "exp"),
        P("ctx", "exp"),
        P("exp"),
        P(),
        P(("ctx", "exp"), None),
        P(("ctx", "exp"), None),
        P("exp", None, "ctx"),
        P("exp", None, "ctx"),
        P("exp", "ctx", None),
    )
    out_specs = P(("ctx", "exp"), None)
    return jax.shard_map(body, mesh=mesh, in_specs=in_specs, out_specs=out_specs, check_vma=False)
```

```python
import functools

import jax
import jax.numpy as jnp
from jax import lax
from jax.experimental import pallas as pl
from jax.experimental.pallas import tpu as pltpu
from jax.sharding import PartitionSpec as P

HEAD = 128
EPSILON = 1e-05
F32 = jnp.float32
BF16 = jnp.bfloat16
LANES = 128
MIB = 2**20


def swap(x, axis, bits):
    n = lax.axis_size(axis)
    return lax.ppermute(x, axis, [(i, i ^ bits) for i in range(n)])


def call(kernel, outs, *args, scratch=(), any_args=(), vmem=12, flops=0, nbytes=0):
    specs = [
        pl.BlockSpec(memory_space=pltpu.HBM if i in any_args else pltpu.VMEM)
        for i in range(len(args))
    ]
    args = [
        pltpu.with_memory_space_constraint(a, pltpu.HBM) if i in any_args else a
        for i, a in enumerate(args)
    ]
    return pl.pallas_call(
        kernel,
        out_shape=tuple(jax.ShapeDtypeStruct(s, d) for s, d in outs),
        in_specs=specs,
        out_specs=tuple(pl.BlockSpec(memory_space=pltpu.VMEM) for _ in outs),
        scratch_shapes=list(scratch),
        compiler_params=pltpu.CompilerParams(vmem_limit_bytes=vmem * MIB),
        cost_estimate=pl.CostEstimate(flops=flops, bytes_accessed=nbytes, transcendentals=0),
    )(*args)


def bit_order(n, turn):
    count = n.bit_length() - 1
    return [(i + turn) % count for i in range(count)] if count else []


def triangle(length, flip):
    row = lax.broadcasted_iota(jnp.int32, (length, length), 0)
    col = lax.broadcasted_iota(jnp.int32, (length, length), 1)
    return (row <= col) if flip else (row >= col)


def front_kernel(n_exp, *refs):
    sources, refs = refs[:8], refs[8:]
    outs, refs = refs[: 5 + n_exp], refs[5 + n_exp :]
    held, sem = refs[:8], refs[8]
    copies = [pltpu.make_async_copy(sources[i], held[i], sem.at[i]) for i in range(8)]
    for copy in copies:
        copy.start()
    decay_ref, key_ref, value_ref, query_ref, ids_ref, route_ref, res_ref, gain_in = held
    state_ref, within_ref, query_out, grow_ref, gain_ref, *share_refs = outs
    heads, length = decay_ref.shape
    causal = triangle(length, False)
    lower = causal.astype(F32)
    upper = triangle(length, True).astype(F32)
    copies[0].wait()
    exact = lax.Precision.HIGHEST
    dims = (((1,), (1,)), ((), ()))
    decay = decay_ref[...]
    down = lax.dot_general(lower, decay, dims, precision=exact, preferred_element_type=F32)
    along = jnp.dot(decay, upper, precision=exact, preferred_element_type=F32)
    copies[1].wait()
    copies[2].wait()
    tail_rows = state_ref.shape[0] - heads * HEAD
    line = lax.broadcasted_iota(jnp.int32, (tail_rows, HEAD), 0)
    tail = jnp.zeros(line.shape, F32)
    grow_lane = lax.broadcasted_iota(jnp.int32, (length, LANES), 1)
    grow = jnp.zeros((length, LANES), F32)
    for h in range(heads):
        part = slice(h * HEAD, (h + 1) * HEAD)
        here = down[:, h : h + 1]
        total = here[length - 1 : length, :]
        weighted = (key_ref[:, part].astype(F32) * jnp.exp(total - here)).astype(BF16)
        state_ref[part, :] = lax.dot_general(
            weighted, value_ref[:, part], (((0,), (0,)), ((), ())), preferred_element_type=F32
        ).astype(BF16)
        wide = jnp.broadcast_to(total, line.shape)
        high = wide.astype(BF16).astype(F32)
        tail = jnp.where(line == 2 * h, high, jnp.where(line == 2 * h + 1, wide - high, tail))
        grow = jnp.where(grow_lane == h, jnp.exp(here), grow)
    state_ref[heads * HEAD :, :] = tail.astype(BF16)
    grow_ref[...] = grow
    for copy in copies[3:]:
        copy.wait()
    gain_ref[...] = gain_in[...]
    query_out[...] = query_ref[...]

    rows = res_ref.shape[0]
    width = res_ref.shape[1] // n_exp
    me = lax.axis_index("exp")
    row = lax.broadcasted_iota(jnp.int32, (rows, rows), 0)
    col = lax.broadcasted_iota(jnp.int32, (rows, rows), 1)
    lane = lax.broadcasted_iota(jnp.int32, (rows, LANES), 1)
    ids = ids_ref[...].astype(F32)
    info = jnp.zeros((rows, LANES), F32)

    def column(line):
        return jnp.sum(jnp.where(row == col, line, 0.0), axis=1, keepdims=True)

    for k in range(2):
        mine = column(ids[k : k + 1, :])
        count = jnp.zeros((rows, rows), F32)
        for other in range(2):
            count = count + ((mine == ids[other : other + 1, :]) & (row > col)).astype(F32)
        slot = jnp.sum(count, axis=1, keepdims=True)
        weight = column(route_ref[k : k + 1, :])
        high = weight.astype(BF16).astype(F32)
        info = jnp.where(lane == k, mine, info)
        info = jnp.where(lane == 2 + k, slot, info)
        info = jnp.where(lane == 4 + k, high, info)
        info = jnp.where(lane == 6 + k, weight - high, info)
    info = info.astype(BF16)
    for rel in range(n_exp):
        start = pl.multiple_of((me ^ rel) * width, LANES)
        share_refs[rel][:, :width] = res_ref[:, pl.ds(start, width)]
        share_refs[rel][:, width:] = info

    for h in range(heads):
        part = slice(h * HEAD, (h + 1) * HEAD)
        scores = lax.dot_general(
            query_ref[:, part], key_ref[:, part], dims, preferred_element_type=F32
        )
        spread = down[:, h : h + 1] - along[h : h + 1, :]
        spread = jnp.exp(jnp.where(causal, spread, -1e30))
        within_ref[:, part] = jnp.dot(
            (scores * spread).astype(BF16), value_ref[:, part], preferred_element_type=F32
        )


def hidden_kernel(n_ctx, n_exp, grow_ref, query_ref, within_ref, gain_ref, *refs):
    states = refs[: n_ctx - 1]
    shares = refs[n_ctx - 1 : n_ctx - 1 + n_exp]
    hid_ref, info_ref, res_ref = refs[n_ctx - 1 + n_exp :]
    width = query_ref.shape[1]
    heads = width // HEAD
    me = lax.axis_index("exp")
    block = lax.axis_index("ctx")
    rows = shares[0].shape[0]
    for rel in range(n_exp):
        start = pl.multiple_of((me ^ rel) * rows, 16)
        res_ref[pl.ds(start, rows), :] = shares[rel][:, :width]
        info_ref[pl.ds(start, rows), :] = shares[rel][:, width:]
    grow = grow_ref[...]
    tails = [s[heads * HEAD :, :].astype(F32) for s in states]
    for h in range(heads):
        part = slice(h * HEAD, (h + 1) * HEAD)
        totals = [t[2 * h : 2 * h + 1, :] + t[2 * h + 1 : 2 * h + 2, :] for t in tails]
        incoming = jnp.zeros((HEAD, HEAD), F32)
        for a in range(1, n_ctx):
            log_weight = jnp.zeros((1, HEAD), F32)
            for b in range(1, n_ctx):
                if b != a:
                    between = ((block ^ b) > (block ^ a)) & ((block ^ b) < block)
                    log_weight = log_weight + totals[b - 1] * jnp.where(between, 1.0, 0.0)
            weight = jnp.exp(log_weight) * jnp.where((block ^ a) < block, 1.0, 0.0)
            incoming = incoming + weight * states[a - 1][part, :].astype(F32)
        carried = grow[:, h : h + 1] * jnp.dot(
            query_ref[:, part], incoming.astype(BF16), preferred_element_type=F32
        )
        raw = carried + within_ref[:, part]
        scale = lax.rsqrt(jnp.mean(raw * raw, axis=-1, keepdims=True) + EPSILON)
        head_out = (raw * scale * gain_ref[:, part]).astype(BF16)
        hid_ref[:, part] = (res_ref[:, part].astype(F32) + head_out.astype(F32)).astype(BF16)


def pack_kernel(n_exp, capacity, tok_rows, hid_ref, other_ref, info_ref, *out_refs):
    nz = n_exp // 2
    *packs, weight_ref = out_refs
    length, width = hid_ref.shape
    slots = packs[0].shape[0]
    me = lax.axis_index("exp")
    info = info_ref[...].astype(F32)
    whole = info.astype(jnp.int32)
    home = lax.broadcasted_iota(jnp.int32, (length, 1), 0) // tok_rows
    lane = lax.broadcasted_iota(jnp.int32, (length, slots), 1)
    for z in range(nz):
        expert = me ^ (2 * z)
        rel = home ^ expert
        base = (rel & 1) * (nz * capacity) + (rel >> 1) * capacity
        chosen = []
        for k in range(2):
            place = jnp.where(whole[:, k : k + 1] == expert, base + whole[:, 2 + k : 3 + k], -1)
            chosen.append((lane == place).astype(F32))
        pick = (chosen[0] + chosen[1]).astype(BF16)
        dims = (((0,), (0,)), ((), ()))
        packs[z][:, :width] = lax.dot_general(
            pick, hid_ref[...], dims, preferred_element_type=F32
        ).astype(BF16)
        packs[z][:, width:] = lax.dot_general(
            pick, other_ref[...], dims, preferred_element_type=F32
        ).astype(BF16)
        if z == 0:
            weights = chosen[0] * (info[:, 4:5] + info[:, 6:7])
            weights = weights + chosen[1] * (info[:, 5:6] + info[:, 7:8])
            weight_ref[...] = lax.dot_general(
                weights,
                jnp.ones((length, LANES), F32),
                dims,
                precision=lax.Precision.HIGHEST,
                preferred_element_type=F32,
            )


def gate_kernel(n_ctx, piece, first, last, gain_ref, gate_ref, up_ref, *refs):
    rows_in = refs[:n_ctx]
    rest = refs[n_ctx:]
    if first:
        prev = None
    else:
        prev, rest = rest[:3], rest[3:]
    if last:
        act_ref, x_ref, gate_buf, up_buf, sem = rest
        outs = None
    else:
        outs = rest[:3]
        x_ref, gate_buf, up_buf, sem = rest[3:]
    me = lax.axis_index("exp")
    slots = rows_in[0].shape[0]
    width = rows_in[0].shape[1] // 2
    copies = []
    for c in range(2):
        start = pl.multiple_of((me ^ (2 * piece + c)) * width, LANES)
        for w_ref, buf, which in ((gate_ref, gate_buf, 0), (up_ref, up_buf, 1)):
            copy = pltpu.make_async_copy(
                w_ref.at[0, pl.ds(start, width), :], buf.at[c], sem.at[2 * c + which]
            )
            copy.start()
            copies.append(copy)
    squares = []
    for r in range(n_ctx):
        total = None
        for c in range(2):
            start = pl.multiple_of((me ^ (2 * piece + c)) * width, LANES)
            gain = gain_ref[:, pl.ds(start, width)]
            x = rows_in[r][:, c * width : (c + 1) * width].astype(F32)
            x_ref[c, r * slots : (r + 1) * slots, :] = (x * gain).astype(BF16)
            square = jnp.sum(x * x, axis=1, keepdims=True)
            total = square if total is None else total + square
        squares.append(jnp.broadcast_to(total, (slots, LANES)))
    for c in range(2):
        x = x_ref[c]
        copies[2 * c].wait()
        gate = jnp.dot(x, gate_buf[c], preferred_element_type=F32)
        gate_sum = gate if c == 0 else gate_sum + gate
        copies[2 * c + 1].wait()
        up = jnp.dot(x, up_buf[c], preferred_element_type=F32)
        up_sum = up if c == 0 else up_sum + up
    square_sum = jnp.concatenate(squares, axis=0)
    if prev is not None:
        gate_sum = gate_sum + prev[0][...]
        up_sum = up_sum + prev[1][...]
        square_sum = square_sum + prev[2][...]
    if last:
        model_width = gain_ref.shape[1]
        scale = lax.rsqrt(square_sum[:, :1] / model_width + EPSILON)
        gate_val = gate_sum * scale
        up_val = up_sum * scale
        act_ref[...] = (gate_val * jax.nn.sigmoid(gate_val) * up_val).astype(BF16)
    else:
        outs[0][...] = gate_sum
        outs[1][...] = up_sum
        outs[2][...] = square_sum


def down_kernel(piece, first_bit, n_ctx, chunks, act_ref, down_ref, send_ref, *refs):
    *keeps, buf, sem = refs
    slots = keeps[0].shape[0]
    width = buf.shape[-1]
    copies = []
    for j in range(chunks):
        start = (piece * chunks + j) * width
        copy = pltpu.make_async_copy(
            down_ref.at[0, :, pl.ds(start, width)], buf.at[j], sem.at[j]
        )
        copy.start()
        copies.append(copy)
    sends = [r for r in range(n_ctx) if r >> first_bit & 1]
    stays = [r for r in range(n_ctx) if not r >> first_bit & 1]
    for j in range(chunks):
        copies[j].wait()
        out = jnp.dot(act_ref[...], buf[j], preferred_element_type=F32).astype(BF16)
        cols = slice(j * width, (j + 1) * width)
        for i, r in enumerate(sends):
            send_ref[i * slots : (i + 1) * slots, cols] = out[r * slots : (r + 1) * slots, :]
        for i, r in enumerate(stays):
            keeps[i][:, cols] = out[r * slots : (r + 1) * slots, :]


def finish_kernel(n_exp, n_parts, terms, first_piece, weight_ref, *refs):
    nz = n_exp // 2
    rows_in = refs[:nz]
    parts = refs[nz : nz + terms * n_parts]
    own_ref, other_ref, rows_ref = refs[nz + terms * n_parts :]
    slots, cols = rows_in[0].shape
    width = cols // 2
    half = slots // 2
    me = lax.axis_index("exp")
    for z in range(nz):
        for c in range(2):
            rows_ref[2 * z + c] = rows_in[z][:, c * width : (c + 1) * width]
    weight = weight_ref[:, :1]
    for i in range(n_parts):
        for c in range(2):
            inner = slice(c * width, (c + 1) * width)
            total = parts[terms * i][:slots, inner].astype(F32)
            for j in range(1, terms):
                total = total + parts[terms * i + j][:slots, inner].astype(F32)
            block = 2 * (first_piece + i) + c
            hid = rows_ref[me ^ block].astype(F32)
            out = (total * weight + 0.5 * hid).astype(BF16)
            outer = slice(i * cols + c * width, i * cols + (c + 1) * width)
            own_ref[:, outer] = out[:half, :]
            other_ref[:, outer] = out[half:, :]


def turn_kernel(nz, capacity, own_ref, other_ref, *refs):
    *outs, both_ref = refs
    half = own_ref.shape[0]
    both_ref[:half, :] = own_ref[...]
    both_ref[half:, :] = other_ref[...]
    line = lax.broadcasted_iota(jnp.int32, (2 * half, 2 * half), 0)
    lane = lax.broadcasted_iota(jnp.int32, (2 * half, 2 * half), 1)
    core = lane // half
    z = (lane % half) // capacity
    s = (lane % half) % capacity
    pick = (line == z * (2 * capacity) + core * capacity + s).astype(BF16)
    moved = jnp.dot(pick, both_ref[...], preferred_element_type=F32).astype(BF16)
    for i in range(nz):
        outs[i][...] = moved[i * 2 * capacity : (i + 1) * 2 * capacity, :]


def home_kernel(nz, groups, capacity, share_ref, *refs):
    *pieces, out_ref = refs
    me = lax.axis_index("exp")
    tok_rows = out_ref.shape[0]
    cols = pieces[0].shape[1]
    width = share_ref.shape[1] - LANES
    info = share_ref[:, width:].astype(F32).astype(jnp.int32)
    lane = lax.broadcasted_iota(jnp.int32, (tok_rows, 2 * capacity), 1)
    picks = []
    for z in range(nz):
        pick = jnp.zeros(lane.shape, F32)
        for k in range(2):
            rel = info[:, k : k + 1] ^ me
            place = jnp.where((rel >> 1) == z, (rel & 1) * capacity + info[:, 2 + k : 3 + k], -1)
            pick = pick + (lane == place).astype(F32)
        picks.append(pick.astype(BF16))
    for g in range(groups):
        total = None
        for z in range(nz):
            term = jnp.dot(picks[z], pieces[g * nz + z][...], preferred_element_type=F32)
            total = term if total is None else total + term
        out_ref[:, g * cols : (g + 1) * cols] = total.astype(BF16)


def gather_ctx(piece, n_ctx, turn):
    held = {0: piece}
    for bit in bit_order(n_ctx, turn):
        for rel in sorted(held):
            held[rel ^ (1 << bit)] = swap(held[rel], "ctx", 1 << bit)
    return [held[r] for r in range(n_ctx)]


def body(
    residual_in,
    query_rows,
    key_rows,
    value_rows,
    log_decay,
    attn_gain,
    moe_gain,
    expert_ids,
    route_weight,
    gate_weight,
    up_weight,
    down_weight,
):
    n_ctx = lax.axis_size("ctx")
    n_exp = lax.axis_size("exp")
    nz = n_exp // 2
    length, width = query_rows.shape
    heads = width // HEAD
    tok_rows, model_width = residual_in.shape
    capacity = 3 * tok_rows // n_exp
    slots = n_exp * capacity
    hidden = gate_weight.shape[2]
    rows = n_ctx * slots
    tail = -(-2 * heads // 16) * 16
    sources = [
        log_decay.T,
        key_rows,
        value_rows,
        query_rows,
        expert_ids.T,
        route_weight.T,
        residual_in,
        attn_gain.reshape(1, width),
    ]
    state, within, query, grow, head_gain, *shares = call(
        functools.partial(front_kernel, n_exp),
        [
            ((heads * HEAD + tail, HEAD), BF16),
            ((length, width), F32),
            ((length, width), BF16),
            ((length, LANES), F32),
            ((1, width), F32),
        ]
        + [((tok_rows, width + LANES), BF16)] * n_exp,
        *sources,
        any_args=range(8),
        scratch=[pltpu.VMEM(x.shape, x.dtype) for x in sources]
        + [pltpu.SemaphoreType.DMA((8,))],
    )
    states = [swap(state, "ctx", r) for r in range(1, n_ctx)]
    moved = [shares[0]] + [swap(shares[r], "exp", r) for r in range(1, n_exp)]
    hid, info = call(
        functools.partial(hidden_kernel, n_ctx, n_exp),
        [((length, width), BF16), ((length, LANES), BF16)],
        grow,
        query,
        within,
        head_gain,
        *states,
        *moved,
        scratch=[pltpu.VMEM((length, width), BF16)],
    )
    hid_other = swap(hid, "exp", 1)
    *packs, row_weight = call(
        functools.partial(pack_kernel, n_exp, capacity, tok_rows),
        [((slots, 2 * width), BF16)] * nz + [((slots, LANES), F32)],
        hid,
        hid_other,
        info,
    )
    arrived = [packs[0]] + [swap(packs[z], "exp", 2 * z) for z in range(1, nz)]
    gathered = [gather_ctx(arrived[z], n_ctx, z) for z in range(nz)]

    gain = moe_gain.reshape(1, model_width)
    sums = ()
    for z in range(nz):
        last = z == nz - 1
        outs = (
            [((rows, hidden), BF16)]
            if last
            else [((rows, hidden), F32), ((rows, hidden), F32), ((rows, LANES), F32)]
        )
        sums = call(
            functools.partial(gate_kernel, n_ctx, z, z == 0, last),
            outs,
            gain,
            gate_weight,
            up_weight,
            *gathered[z],
            *sums,
            any_args=(1, 2),
            scratch=[
                pltpu.VMEM((2, rows, width), BF16),
                pltpu.VMEM((2, width, hidden), BF16),
                pltpu.VMEM((2, width, hidden), BF16),
                pltpu.SemaphoreType.DMA((4,)),
            ],
            vmem=20,
            flops=8 * rows * width * hidden,
            nbytes=8 * width * hidden,
        )
    (act,) = sums

    chunks = 2
    finished = []
    for p in range(nz):
        order = bit_order(n_ctx, p)
        stays = [r for r in range(n_ctx) if not r >> order[0] & 1]
        send, *keeps = call(
            functools.partial(down_kernel, p, order[0], n_ctx, chunks),
            [((rows // 2, 2 * width), BF16)] + [((slots, 2 * width), BF16)] * (n_ctx // 2),
            act,
            down_weight,
            any_args=(1,),
            scratch=[
                pltpu.VMEM((chunks, hidden, 2 * width // chunks), BF16),
                pltpu.SemaphoreType.DMA((chunks,)),
            ],
            flops=4 * rows * width * hidden,
            nbytes=4 * width * hidden,
        )
        got = swap(send, "ctx", 1 << order[0])
        held = {r: [keeps[i], got[i * slots : (i + 1) * slots]] for i, r in enumerate(stays)}
        held[0][1] = got
        for bit in order[1:]:
            moving = [r for r in sorted(held) if r >> bit & 1]
            outgoing = [
                functools.reduce(jnp.add, [t.astype(F32) for t in held.pop(r)]).astype(BF16)
                for r in moving
            ]
            packed = outgoing[0] if len(outgoing) == 1 else jnp.concatenate(outgoing, axis=0)
            got = swap(packed, "ctx", 1 << bit)
            for i, r in enumerate(moving):
                kept = r ^ (1 << bit)
                held[kept].append(got if kept == 0 else got[i * slots : (i + 1) * slots])
        finished.append(held[0])

    groups = 2
    per = nz // groups
    pieces = []
    for g in range(groups):
        parts = [t for p in range(g * per, (g + 1) * per) for t in finished[p]]
        terms = len(finished[0])
        own, other = call(
            functools.partial(finish_kernel, n_exp, per, terms, g * per),
            [((slots // 2, per * 2 * width), BF16)] * 2,
            row_weight,
            *arrived,
            *parts,
            scratch=[pltpu.VMEM((n_exp, slots, width), BF16)],
        )
        other = swap(other, "exp", 1)
        turned = call(
            functools.partial(turn_kernel, nz, capacity),
            [((2 * capacity, per * 2 * width), BF16)] * nz,
            own,
            other,
            scratch=[pltpu.VMEM((slots, per * 2 * width), BF16)],
        )
        pieces += [turned[0]] + [swap(turned[z], "exp", 2 * z) for z in range(1, nz)]
    (out,) = call(
        functools.partial(home_kernel, nz, groups, capacity),
        [((tok_rows, model_width), BF16)],
        shares[0],
        *pieces,
    )
    return out


def solution(mesh):
    in_specs = (
        P(("ctx", "exp"), None),
        P("ctx", "exp"),
        P("ctx", "exp"),
        P("ctx", "exp"),
        P("ctx", "exp"),
        P("exp"),
        P(),
        P(("ctx", "exp"), None),
        P(("ctx", "exp"), None),
        P("exp", None, "ctx"),
        P("exp", None, "ctx"),
        P("exp", "ctx", None),
    )
    out_specs = P(("ctx", "exp"), None)
    return jax.shard_map(body, mesh=mesh, in_specs=in_specs, out_specs=out_specs, check_vma=False)
```
